32 devices in a mesh: rep: 4 (over y, core), tp: 8 (over z, x).
Axes of the slice: x: 2, y: 2, z: 4, core: 2. Of those that a mesh axis runs over, the one named last changes fastest.
Arguments:
- inputs: bfloat16 [16384, 1024], P(('rep', 'tp')), may hold values from -6 to 6
- cotangent: bfloat16 [16384, 8192], P('rep', 'tp'), may hold values from -1 to 1
- master: float32 [1024, 8192], P('rep', 'tp'), may hold values from -6 to 6
- moment: float32 [1024, 8192], P('rep', 'tp'), may hold values from -6 to 6
- second: float32 [1024, 8192], P('rep', 'tp'), may hold values from 0.5 to 4
Outputs:
- combined: float32 [1024, 8192], P('rep', 'tp')
- moment_new: float32 [1024, 8192], P('rep', 'tp')
- second_new: float32 [1024, 8192], P('rep', 'tp')
- master_new: float32 [1024, 8192], P('rep', 'tp')
- weights: bfloat16 [1024, 8192], P(None, 'tp')
The draws below stay inside these ranges and needn't reach their ends.
All inputs are finite; a program needn't handle non-finite values.
Results may differ from the reference program's by a relative error of at most 0.001.
Values may be sent and summed in bfloat16 or wider, within the bound.
A program may use at most 64 MiB of HBM per device.

```python
import math
import jax
import jax.numpy as jnp
from jax import lax

D = 1024
F = 8192
TOK_DEV = 4096
TOKENS = 16384
LEVELS = 2
N_REP = 4


def replica_mix(key, seed_offset):
    replica_count = TOKENS // TOK_DEV
    shared_weight = jax.random.uniform(jax.random.fold_in(key, seed_offset), (replica_count,), jnp.float32, 0.1, 0.95)
    replica_scale = jnp.exp(jax.random.uniform(jax.random.fold_in(key, seed_offset + 1), (replica_count,), jnp.float32, -0.7, 0.7))
    rows_weight = jnp.repeat(shared_weight, TOK_DEV)[:, None]
    rows_scale = jnp.repeat(replica_scale, TOK_DEV)[:, None]
    return (rows_weight, rows_scale)


def mixed_rows(key, width, seed_offset, column_factor):
    rows_weight, rows_scale = replica_mix(key, seed_offset + 5)
    shared = jax.random.normal(jax.random.fold_in(key, seed_offset), (TOK_DEV, width), jnp.float32)
    single = jax.random.normal(jax.random.fold_in(key, seed_offset + 1), (TOKENS, width), jnp.float32)
    mixing = rows_weight * column_factor[None, :]
    rest_weight = jnp.sqrt(1.0 - mixing * mixing)
    tiled = jnp.tile(shared, (TOKENS // TOK_DEV, 1))
    return rows_scale * (mixing * tiled + rest_weight * single)


def draw_inputs(key, part):
    values = mixed_rows(key, D, 11, jnp.ones((D,), jnp.float32))
    return jnp.clip(values, -6.0, 6.0).astype(jnp.bfloat16)


def draw_cotangent(key, part):
    position = jnp.arange(F, dtype=jnp.float32) / F
    column_scale = (0.5 + position) * TOK_DEV ** (-0.5)
    column_factor = 0.1 + 0.9 * position
    values = mixed_rows(key, F, 31, column_factor)
    return jnp.clip(values * column_scale[None, :], -1.0, 1.0).astype(jnp.bfloat16)


def block_levels(rng, dims, cuts, smallest, high):
    def one(axis_at, parts):
        steps = jax.random.uniform(jax.random.fold_in(jax.random.fold_in(rng, 6), axis_at), (parts,), jnp.float32, smallest / len(cuts), high / len(cuts))
        return jnp.repeat(jnp.exp(steps), dims[axis_at] // parts).reshape((-1,) + (1,) * (len(dims) - axis_at - 1))

    level = one(*cuts[0])
    for cut in cuts[1:]:
        level = level * one(*cut)
    return level


def scatter_about(rng, shape, scale, bound, shards=(), kind=jnp.bfloat16):
    drawn = scale * jax.random.normal(rng, shape, jnp.float32)
    if shards:
        drawn = drawn * block_levels(rng, shape, shards, -0.22, 0.18)
    return jnp.clip(drawn, -bound, bound).astype(kind)


def setup_inputs(seed: int = 0) -> dict:
    key_list = jax.random.split(jax.random.key(seed), 6)
    inputs = draw_inputs(jax.random.fold_in(key_list[5], 71), 0)
    cotangent = draw_cotangent(jax.random.fold_in(key_list[5], 71), 0)
    master = scatter_about(key_list[2], (D, F), 1.0, 6.0, ((0, 4), (1, 8)), jnp.float32)
    moment = scatter_about(key_list[3], (D, F), 1.0, 6.0, ((0, 4), (1, 8)), jnp.float32)
    second = jnp.clip(jnp.exp(math.log(4.0) - 2.0794415 * jax.random.uniform(key_list[4], (D, F), jnp.float32) ** block_levels(key_list[4], (D, F), ((0, 4), (1, 8)), -0.2, 0.2)), 0.5, 4.0)
    return dict(inputs=inputs, cotangent=cotangent, master=master, moment=moment, second=second)


EPS_SUM = 1e-06
BETA_ONE = 0.9
BETA_TWO = 0.999
LEARN = 0.01
CORRECT_ONE = 1.0 - 0.9 ** 50
CORRECT_TWO = 1.0 - 0.999 ** 50

def reference(inputs, cotangent, master, moment, second):
    tokens_all = inputs.reshape(N_REP, TOK_DEV, D)
    cotan_all = cotangent.reshape(N_REP, TOK_DEV, F)

    def replica_grad(pair):
        return lax.dot_general(pair[0], pair[1], (((0,), (0,)), ((), ())), preferred_element_type=jnp.float32)
    gradients = lax.map(replica_grad, (tokens_all, cotan_all))
    for level_index in range(LEVELS):
        half_count = gradients.shape[0] // 2
        lower_half = gradients[:half_count]
        upper_half = gradients[half_count:]
        low_low = lax.optimization_barrier(jnp.sum(lower_half * lower_half, axis=(1, 2)))
        high_high = lax.optimization_barrier(jnp.sum(upper_half * upper_half, axis=(1, 2)))
        cross_term = lax.optimization_barrier(jnp.sum(lower_half * upper_half, axis=(1, 2)))
        lower_coef = 1.0 - cross_term / (2.0 * (low_low + EPS_SUM))
        upper_coef = 1.0 - cross_term / (2.0 * (high_high + EPS_SUM))
        gradients = lower_coef[:, None, None] * lower_half + upper_coef[:, None, None] * upper_half
    combined = gradients[0]
    moment_new = BETA_ONE * moment + (1.0 - BETA_ONE) * combined
    second_new = BETA_TWO * second + (1.0 - BETA_TWO) * combined * combined
    master_new = master - LEARN * (moment_new / CORRECT_ONE) / (jnp.sqrt(second_new / CORRECT_TWO) + 1e-08)
    return (combined, moment_new, second_new, master_new, master_new.astype(jnp.bfloat16))
```

```python
import functools
import jax
import jax.numpy as jnp
from jax import lax
from jax.experimental import pallas as pl
from jax.experimental.pallas import tpu as pltpu
from jax.sharding import PartitionSpec as P

EPS_SUM = 1e-06
BETA_ONE = 0.9
BETA_TWO = 0.999
LEARN = 0.01
CORRECT_ONE = 1.0 - 0.9**50
CORRECT_TWO = 1.0 - 0.999**50
LANES = 128
SUBLANES = 8
PIECES = 4
OWN_LEAD = 2
MESH = pl.DeviceIdType.MESH


def adasum_weights(gram, replicas):
    entries = [{s: jnp.ones((1, 1), jnp.float32)} for s in range(replicas)]

    def inner(left, right):
        total = None
        for i, u in left.items():
            for j, v in right.items():
                term = (u * v) * gram[min(i, j), max(i, j)]
                total = term if total is None else total + term
        return total

    while len(entries) > 1:
        half = len(entries) // 2
        merged = []
        for a, b in zip(entries[:half], entries[half:]):
            aa, bb, ab = inner(a, a), inner(b, b), inner(a, b)
            ca = 1.0 - ab / (2.0 * (aa + EPS_SUM))
            cb = 1.0 - ab / (2.0 * (bb + EPS_SUM))
            merged.append({**{i: ca * u for i, u in a.items()}, **{i: cb * u for i, u in b.items()}})
        entries = merged
    return entries[0]


def kernel(
    replicas, outer, inner,
    x_hbm, g_hbm, master_hbm, moment_hbm, second_hbm,
    comb_hbm, mom_hbm, sec_hbm, mas_hbm, w_hbm,
    xg, cot, gsend, gr, master, moment, second, comb, mom, sec, mas, wb, tile_tp, tile_rep,
    load_x, load_g, load_s, x_send, x_recv, g_send, g_recv, t_send, t_recv, r_send, r_recv, w_send, w_recv, out_sem,
):
    rep = lax.axis_index("rep")
    tp = lax.axis_index("tp")
    peers = outer * inner
    i, j = tp // inner, tp % inner
    chunks = xg.shape[0]
    width = xg.shape[3]
    tokens = xg.shape[2]
    per_segment = chunks // replicas
    segment_order = list(range(replicas - 1, -1, -1))
    rows = gr.shape[1]

    loads = []
    for k in range(chunks):
        s, h = segment_order[k // per_segment], k % per_segment
        column = pl.multiple_of(((rep ^ s) * per_segment + h) * width, width)
        loads.append(pltpu.make_async_copy(x_hbm.at[:, pl.ds(column, width)], xg.at[k, tp], load_x.at[k]))
    for copy in loads:
        copy.start()
    load_cot = pltpu.make_async_copy(g_hbm, cot, load_g)
    load_cot.start()
    state_loads = [
        pltpu.make_async_copy(src, dst, load_s.at[n])
        for n, (src, dst) in enumerate(((master_hbm, master), (moment_hbm, moment), (second_hbm, second)))
    ]
    for copy in state_loads:
        copy.start()

    barrier = pltpu.get_barrier_semaphore()
    for d in range(1, peers):
        pl.semaphore_signal(barrier, inc=1, device_id=(rep, (tp + d) % peers), device_id_type=MESH)
    for s in range(1, replicas):
        pl.semaphore_signal(barrier, inc=1, device_id=(rep ^ s, tp), device_id_type=MESH)
    pl.semaphore_wait(barrier, peers - 1 + replicas - 1)

    pending = []

    def send(k, slot, direction, cond, to_i, to_j):
        target = jnp.clip(to_i, 0, outer - 1) * inner + jnp.clip(to_j, 0, inner - 1)
        copy = pltpu.make_async_remote_copy(
            xg.at[k, slot], xg.at[k, slot], x_send.at[k, direction, slot], x_recv.at[k, slot],
            device_id=(rep, target), device_id_type=MESH,
        )

        @pl.when(cond)
        def _():
            copy.start()

        pending.append((cond, copy))

    def wait_block(k, slot):
        pltpu.make_async_remote_copy(
            xg.at[k, slot], xg.at[k, slot], x_send.at[k, 0, slot], x_recv.at[k, slot],
            device_id=(rep, tp), device_id_type=MESH,
        ).wait_recv()

    def route(k):
        swap = k % 4 == 1
        if swap:
            n1, n2, p1, p2 = inner, outer, j, i
            slot_of = lambda q1, q2: q2 * inner + q1
            place = lambda q1, q2: (q2, q1)
        else:
            n1, n2, p1, p2 = outer, inner, i, j
            slot_of = lambda q1, q2: q1 * inner + q2
            place = lambda q1, q2: (q1, q2)
        return n1, n2, p1, p2, slot_of, place

    def cross(k, slot, cond, n2, p1, p2, place):
        up = p2 + 1 < n2
        down = p2 - 1 >= 0
        if cond is not None:
            up, down = cond & up, cond & down
        send(k, slot, 2, up, *place(p1, p2 + 1))
        send(k, slot, 3, down, *place(p1, p2 - 1))

    def own(k):
        n1, n2, p1, p2, slot_of, place = route(k)
        loads[k].wait()
        send(k, tp, 0, p1 + 1 < n1, *place(p1 + 1, p2))
        send(k, tp, 1, p1 - 1 >= 0, *place(p1 - 1, p2))
        cross(k, tp, None, n2, p1, p2, place)

    def first_line(k):
        n1, n2, p1, p2, slot_of, place = route(k)
        for t in range(1, n1):
            for step in (-1, 1):
                origin = p1 + step * t
                valid = (origin >= 0) & (origin < n1)
                slot = slot_of(jnp.clip(origin, 0, n1 - 1), p2)

                @pl.when(valid)
                def _():
                    wait_block(k, slot)

                onward = p1 - step
                send(k, slot, 0 if step < 0 else 1, valid & (onward >= 0) & (onward < n1), *place(onward, p2))
                cross(k, slot, valid, n2, p1, p2, place)

    def second_line(k):
        n1, n2, p1, p2, slot_of, place = route(k)
        for u in range(1, n2):
            for step in (-1, 1):
                origin = p2 + step * u
                valid = (origin >= 0) & (origin < n2)
                onward = p2 - step
                go = valid & (onward >= 0) & (onward < n2)
                for r in range(n1):
                    slot = slot_of((p1 + r) % n1, jnp.clip(origin, 0, n2 - 1))

                    @pl.when(valid)
                    def _():
                        wait_block(k, slot)

                    if n2 > 2:
                        send(k, slot, 2 if step < 0 else 3, go, *place(p1, onward))

    grad_sends = []

    def consume(k):
        s, h = segment_order[k // per_segment], k % per_segment
        at = pl.ds(h * width, width)
        target = gsend.at[s - 1, at] if s else gr.at[0, at]

        def accumulate(slot, carry):
            part = lax.dot_general(
                xg[k, slot], cot[pl.ds(pl.multiple_of(slot * tokens, tokens), tokens), :],
                (((0,), (0,)), ((), ())), preferred_element_type=jnp.float32,
            )
            target[...] = target[...] + part
            return carry

        target[...] = lax.dot_general(
            xg[k, 0], cot[pl.ds(0, tokens), :], (((0,), (0,)), ((), ())), preferred_element_type=jnp.float32
        )
        lax.fori_loop(1, peers, accumulate, 0)
        if s:
            copy = pltpu.make_async_remote_copy(
                gsend.at[s - 1, at], gr.at[s, at], g_send.at[s - 1, h], g_recv.at[s - 1, h],
                device_id=(rep ^ s, tp), device_id_type=MESH,
            )
            copy.start()
            grad_sends.append(copy)

    for k in range(min(OWN_LEAD, chunks)):
        own(k)
    first_line(0)
    load_cot.wait()
    for k in range(chunks):
        if k + OWN_LEAD < chunks:
            own(k + OWN_LEAD)
        if k + 1 < chunks:
            first_line(k + 1)
        second_line(k)
        consume(k)
    for copy in grad_sends:
        copy.wait_recv()

    pairs = [(s, t) for s in range(replicas) for t in range(s, replicas)]
    fold = gr.shape[2] // LANES

    def products(n, sums):
        block = [gr[s, pl.ds(pl.multiple_of(n * SUBLANES, SUBLANES), SUBLANES), :] for s in range(replicas)]
        out = []
        for total, (s, t) in zip(sums, pairs):
            prod = block[s] * block[t]
            part = prod[:, :LANES]
            for f in range(1, fold):
                part = part + prod[:, f * LANES : (f + 1) * LANES]
            out.append(total + part)
        return tuple(out)

    sums = lax.fori_loop(
        0, rows // SUBLANES, products, tuple(jnp.zeros((SUBLANES, LANES), jnp.float32) for _ in pairs)
    )
    lane = lax.broadcasted_iota(jnp.int32, (SUBLANES, LANES), 1)
    packed = jnp.zeros((SUBLANES, LANES), jnp.float32)
    for n, total in enumerate(sums):
        packed = jnp.where(lane == n, jnp.sum(total, axis=1, keepdims=True), packed)
    tile_tp[0] = packed
    tile_sends = []
    for d in range(1, peers):
        copy = pltpu.make_async_remote_copy(
            tile_tp.at[0], tile_tp.at[d], t_send.at[d - 1], t_recv.at[d - 1],
            device_id=(rep, (tp + d) % peers), device_id_type=MESH,
        )
        copy.start()
        tile_sends.append(copy)
    for copy in state_loads:
        copy.wait()
    for copy in tile_sends:
        copy.wait_recv()
    packed = tile_tp[0]
    for d in range(1, peers):
        packed = packed + tile_tp[d]
    tile_rep[0] = packed
    for s in range(1, replicas):
        copy = pltpu.make_async_remote_copy(
            tile_rep.at[0], tile_rep.at[s], r_send.at[s - 1], r_recv.at[s - 1],
            device_id=(rep ^ s, tp), device_id_type=MESH,
        )
        copy.start()
        tile_sends.append(copy)
    for copy in tile_sends[peers - 1 :]:
        copy.wait_recv()
    index = {pair: n for n, pair in enumerate(pairs)}
    seen = [tile_rep[s] for s in range(replicas)]
    gram = {}
    for s, t in pairs:
        value = None
        for d in range(replicas):
            p, q = s ^ d, t ^ d
            picked = jnp.where(lane == index[min(p, q), max(p, q)], seen[d], 0.0)
            value = picked if value is None else value + picked
        gram[s, t] = jnp.sum(value, keepdims=True)
    coef = adasum_weights(gram, replicas)
    coef = [jnp.broadcast_to(coef[s], (SUBLANES, gr.shape[2])) for s in range(replicas)]

    masks = []
    mask = replicas // 2
    while mask:
        masks.append(mask)
        mask //= 2
    piece = rows // PIECES
    outs = []
    w_copies = {}

    def w_send_start(step, s, q):
        m = masks[step]
        at = pl.ds(q * piece, piece)
        copy = pltpu.make_async_remote_copy(
            wb.at[s, at], wb.at[s ^ m, at], w_send.at[s ^ m, q], w_recv.at[s ^ m, q],
            device_id=(rep ^ m, tp), device_id_type=MESH,
        )
        copy.start()
        w_copies[s ^ m, q] = copy

    def put(src, dst, n):
        copy = pltpu.make_async_copy(src, dst, out_sem.at[n])
        copy.start()
        outs.append(copy)

    for q in range(PIECES):
        def update(n, carry):
            at = pl.ds(pl.multiple_of(q * piece + n * SUBLANES * 2, SUBLANES * 2), SUBLANES * 2)
            value = None
            for s in range(replicas):
                term = coef[s][:1] * gr[s, at, :]
                value = term if value is None else value + term
            moment_new = BETA_ONE * moment[at, :] + (1.0 - BETA_ONE) * value
            second_new = BETA_TWO * second[at, :] + (1.0 - BETA_TWO) * value * value
            master_new = master[at, :] - LEARN * (moment_new / CORRECT_ONE) / (
                jnp.sqrt(second_new / CORRECT_TWO) + 1e-08
            )
            comb[at, :] = value
            mom[at, :] = moment_new
            sec[at, :] = second_new
            mas[at, :] = master_new
            wb[0, at, :] = master_new.astype(jnp.bfloat16)
            return carry

        lax.fori_loop(0, piece // (SUBLANES * 2), update, 0)
        for step in range(len(masks)):
            w_send_start(step, 0, q)
    for n, (src, dst) in enumerate(((comb, comb_hbm), (mom, mom_hbm), (sec, sec_hbm), (mas, mas_hbm))):
        put(src, dst, n)
    put(wb.at[0], w_hbm.at[pl.ds(pl.multiple_of(rep * rows, rows), rows)], 4)

    def relay(q, step, s):
        w_copies[s, q].wait_recv()
        for later in range(step + 1, len(masks)):
            w_send_start(later, s, q)

    held = [0]
    for step, m in enumerate(masks):
        fresh = [s ^ m for s in held]
        for q in range(PIECES):
            for s in fresh:
                relay(q, step, s)
        for s in fresh:
            put(wb.at[s], w_hbm.at[pl.ds(pl.multiple_of((rep ^ s) * rows, rows), rows)], 4 + s)
        held = held + fresh

    for cond, copy in pending:
        @pl.when(cond)
        def _():
            copy.wait_send()
    for copy in grad_sends + tile_sends + list(w_copies.values()):
        copy.wait_send()
    for copy in outs:
        copy.wait()


def per_device(inputs, cotangent, master, moment, second):
    replicas = lax.axis_size("rep")
    peers = lax.axis_size("tp")
    inner = 1 << (peers.bit_length() - 1) // 2
    outer = peers // inner
    tokens, depth = inputs.shape
    features = cotangent.shape[1]
    rows = depth // replicas
    width = min(LANES, rows)
    chunks = depth // width
    per_segment = rows // width
    shard = jax.ShapeDtypeStruct((rows, features), jnp.float32)
    anywhere = pl.BlockSpec(memory_space=pl.ANY)
    dma = pltpu.SemaphoreType.DMA
    small = pltpu.VMEM((rows, features), jnp.float32)
    return pl.pallas_call(
        functools.partial(kernel, replicas, outer, inner),
        out_shape=(shard, shard, shard, shard, jax.ShapeDtypeStruct((depth, features), jnp.bfloat16)),
        in_specs=[anywhere] * 5,
        out_specs=(anywhere,) * 5,
        scratch_shapes=[
            pltpu.VMEM((chunks, peers, tokens, width), jnp.bfloat16),
            pltpu.VMEM(cotangent.shape, jnp.bfloat16),
            pltpu.VMEM((replicas - 1, rows, features), jnp.float32),
            pltpu.VMEM((replicas, rows, features), jnp.float32),
            small, small, small, small, small, small, small,
            pltpu.VMEM((replicas, rows, features), jnp.bfloat16),
            pltpu.VMEM((peers, SUBLANES, LANES), jnp.float32),
            pltpu.VMEM((replicas, SUBLANES, LANES), jnp.float32),
            dma((chunks,)),
            dma,
            dma((3,)),
            dma((chunks, 4, peers)),
            dma((chunks, peers)),
            dma((replicas - 1, per_segment)),
            dma((replicas - 1, per_segment)),
            dma((peers - 1,)),
            dma((peers - 1,)),
            dma((replicas - 1,)),
            dma((replicas - 1,)),
            dma((replicas, PIECES)),
            dma((replicas, PIECES)),
            dma((4 + replicas,)),
        ],
        compiler_params=pltpu.CompilerParams(
            collective_id=0, has_side_effects=True, vmem_limit_bytes=60 * 1024 * 1024
        ),
        name="adasum_adam",
    )(inputs, cotangent, master, moment, second)


def solution(mesh):
    return jax.shard_map(
        per_device,
        mesh=mesh,
        in_specs=(
            P(("rep", "tp"), None),
            P("rep", "tp"),
            P("rep", "tp"),
            P("rep", "tp"),
            P("rep", "tp"),
        ),
        out_specs=(P("rep", "tp"), P("rep", "tp"), P("rep", "tp"), P("rep", "tp"), P(None, "tp")),
        check_vma=False,
    )
```

```python
import functools
import jax
import jax.numpy as jnp
from jax import lax
from jax.experimental import pallas as pl
from jax.experimental.pallas import tpu as pltpu
from jax.sharding import PartitionSpec as P

EPS_SUM = 1e-06
BETA_ONE = 0.9
BETA_TWO = 0.999
LEARN = 0.01
CORRECT_ONE = 1.0 - 0.9**50
CORRECT_TWO = 1.0 - 0.999**50
LANES = 128
SUBLANES = 8
PIECES = 4
SPLIT = 2
OWN_LEAD = 9
LINE_LEAD = 6
INNER_FIRST = 5
MESH = pl.DeviceIdType.MESH


def adasum_weights(gram, replicas):
    entries = [{s: jnp.ones((1, 1), jnp.float32)} for s in range(replicas)]

    def inner(left, right):
        total = None
        for i, u in left.items():
            for j, v in right.items():
                term = (u * v) * gram[min(i, j), max(i, j)]
                total = term if total is None else total + term
        return total

    while len(entries) > 1:
        half = len(entries) // 2
        merged = []
        for a, b in zip(entries[:half], entries[half:]):
            aa, bb, ab = inner(a, a), inner(b, b), inner(a, b)
            ca = 1.0 - ab / (2.0 * (aa + EPS_SUM))
            cb = 1.0 - ab / (2.0 * (bb + EPS_SUM))
            merged.append({**{i: ca * u for i, u in a.items()}, **{i: cb * u for i, u in b.items()}})
        entries = merged
    return entries[0]


def kernel(
    replicas, outer, inner,
    x_hbm, g_hbm, master_hbm, moment_hbm, second_hbm,
    comb_hbm, mom_hbm, sec_hbm, mas_hbm, w_hbm,
    xg, cot, gsend, gr, master, moment, second, comb, mom, sec, mas, wb, tile_tp, tile_rep,
    load_x, load_g, load_s, x_send, x_recv, g_send, g_recv, t_send, t_recv, r_send, r_recv, w_send, w_recv, out_sem,
):
    rep = lax.axis_index("rep")
    tp = lax.axis_index("tp")
    peers = outer * inner
    i, j = tp // inner, tp % inner
    units = xg.shape[0]
    width = xg.shape[3]
    tokens = xg.shape[2]
    chunks = units // SPLIT
    per_segment = chunks // replicas
    segment_order = list(range(replicas - 1, -1, -1))
    rows = gr.shape[1]

    loads = []
    for k in range(units):
        c, part = k // SPLIT, k % SPLIT
        s, h = segment_order[c // per_segment], c % per_segment
        column = pl.multiple_of(((rep ^ s) * per_segment + h) * width, width)
        source = x_hbm.at[pl.ds(part * tokens, tokens), pl.ds(column, width)]
        loads.append(pltpu.make_async_copy(source, xg.at[k, tp], load_x.at[k]))
    for copy in loads:
        copy.start()
    cot_loads = []
    for part in range(SPLIT):
        for slot in range(peers):
            source = g_hbm.at[pl.ds((slot * SPLIT + part) * tokens, tokens)]
            cot_loads.append(pltpu.make_async_copy(source, cot.at[part, pl.ds(slot * tokens, tokens)], load_g.at[part, slot]))
    for copy in cot_loads:
        copy.start()
    state_loads = [
        pltpu.make_async_copy(src, dst, load_s.at[n])
        for n, (src, dst) in enumerate(((master_hbm, master), (moment_hbm, moment), (second_hbm, second)))
    ]
    for copy in state_loads:
        copy.start()

    barrier = pltpu.get_barrier_semaphore()
    for d in range(1, peers):
        pl.semaphore_signal(barrier, inc=1, device_id=(rep, (tp + d) % peers), device_id_type=MESH)
    for s in range(1, replicas):
        pl.semaphore_signal(barrier, inc=1, device_id=(rep ^ s, tp), device_id_type=MESH)
    pl.semaphore_wait(barrier, peers - 1 + replicas - 1)

    pending = []

    def send(k, slot, direction, cond, to_i, to_j):
        target = jnp.clip(to_i, 0, outer - 1) * inner + jnp.clip(to_j, 0, inner - 1)
        copy = pltpu.make_async_remote_copy(
            xg.at[k, slot], xg.at[k, slot], x_send.at[k, direction, slot], x_recv.at[k, slot],
            device_id=(rep, target), device_id_type=MESH,
        )

        @pl.when(cond)
        def _():
            copy.start()

        pending.append((cond, copy))

    def wait_block(k, slot):
        pltpu.make_async_remote_copy(
            xg.at[k, slot], xg.at[k, slot], x_send.at[k, 0, slot], x_recv.at[k, slot],
            device_id=(rep, tp), device_id_type=MESH,
        ).wait_recv()

    def route(k):
        swap = k % INNER_FIRST == 1
        if swap:
            n1, n2, p1, p2 = inner, outer, j, i
            slot_of = lambda q1, q2: q2 * inner + q1
            place = lambda q1, q2: (q2, q1)
        else:
            n1, n2, p1, p2 = outer, inner, i, j
            slot_of = lambda q1, q2: q1 * inner + q2
            place = lambda q1, q2: (q1, q2)
        return n1, n2, p1, p2, slot_of, place

    def cross(k, slot, cond, n2, p1, p2, place):
        up = p2 + 1 < n2
        down = p2 - 1 >= 0
        if cond is not None:
            up, down = cond & up, cond & down
        send(k, slot, 2, up, *place(p1, p2 + 1))
        send(k, slot, 3, down, *place(p1, p2 - 1))

    def own(k):
        n1, n2, p1, p2, slot_of, place = route(k)
        loads[k].wait()
        send(k, tp, 0, p1 + 1 < n1, *place(p1 + 1, p2))
        send(k, tp, 1, p1 - 1 >= 0, *place(p1 - 1, p2))
        cross(k, tp, None, n2, p1, p2, place)

    def first_line(k):
        n1, n2, p1, p2, slot_of, place = route(k)
        for t in range(1, n1):
            for step in (-1, 1):
                origin = p1 + step * t
                valid = (origin >= 0) & (origin < n1)
                slot = slot_of(jnp.clip(origin, 0, n1 - 1), p2)

                @pl.when(valid)
                def _():
                    wait_block(k, slot)

                onward = p1 - step
                send(k, slot, 0 if step < 0 else 1, valid & (onward >= 0) & (onward < n1), *place(onward, p2))
                cross(k, slot, valid, n2, p1, p2, place)

    def second_line(k):
        n1, n2, p1, p2, slot_of, place = route(k)
        for u in range(1, n2):
            for step in (-1, 1):
                origin = p2 + step * u
                valid = (origin >= 0) & (origin < n2)
                onward = p2 - step
                go = valid & (onward >= 0) & (onward < n2)
                for r in range(n1):
                    slot = slot_of((p1 + r) % n1, jnp.clip(origin, 0, n2 - 1))

                    @pl.when(valid)
                    def _():
                        wait_block(k, slot)

                    if n2 > 2:
                        send(k, slot, 2 if step < 0 else 3, go, *place(p1, onward))

    grad_sends = []

    def consume(k):
        c, part = k // SPLIT, k % SPLIT
        s, h = segment_order[c // per_segment], c % per_segment
        at = pl.ds(h * width, width)
        target = gsend.at[s - 1, at] if s else gr.at[0, at]
        product = lax.dot_general(
            xg[k].reshape(peers * tokens, width), cot[part],
            (((0,), (0,)), ((), ())), preferred_element_type=jnp.float32,
        )
        target[...] = target[...] + product if part else product
        if s and part == SPLIT - 1:
            copy = pltpu.make_async_remote_copy(
                gsend.at[s - 1, at], gr.at[s, at], g_send.at[s - 1, h], g_recv.at[s - 1, h],
                device_id=(rep ^ s, tp), device_id_type=MESH,
            )
            copy.start()
            grad_sends.append((h, copy))

    pairs = [(s, t) for s in range(replicas) for t in range(s, replicas)]
    fold = gr.shape[2] // LANES

    def inner_products(h, sums):
        for at_h, copy in grad_sends:
            if at_h == h:
                copy.wait_recv()

        def products(n, sums):
            at = pl.ds(pl.multiple_of(h * width + n * SUBLANES, SUBLANES), SUBLANES)
            block = [gr[s, at, :] for s in range(replicas)]
            out = []
            for total, (s, t) in zip(sums, pairs):
                prod = block[s] * block[t]
                part = prod[:, :LANES]
                for f in range(1, fold):
                    part = part + prod[:, f * LANES : (f + 1) * LANES]
                out.append(total + part)
            return tuple(out)

        return lax.fori_loop(0, width // SUBLANES, products, sums)

    sums = tuple(jnp.zeros((SUBLANES, LANES), jnp.float32) for _ in pairs)
    for k in range(min(OWN_LEAD, units)):
        own(k)
    for k in range(min(LINE_LEAD, units)):
        first_line(k)
    for copy in cot_loads:
        copy.wait()
    for k in range(units):
        if k + OWN_LEAD < units:
            own(k + OWN_LEAD)
        if k + LINE_LEAD < units:
            first_line(k + LINE_LEAD)
        second_line(k)
        if k == units - 1:
            for h in range(per_segment - 1):
                sums = inner_products(h, sums)
        consume(k)
    sums = inner_products(per_segment - 1, sums)
    seg_sends = [copy for _, copy in grad_sends]
    lane = lax.broadcasted_iota(jnp.int32, (SUBLANES, LANES), 1)
    packed = jnp.zeros((SUBLANES, LANES), jnp.float32)
    for n, total in enumerate(sums):
        packed = jnp.where(lane == n, jnp.sum(total, axis=1, keepdims=True), packed)
    tile_tp[0] = packed
    tile_sends = []
    for d in range(1, peers):
        copy = pltpu.make_async_remote_copy(
            tile_tp.at[0], tile_tp.at[d], t_send.at[d - 1], t_recv.at[d - 1],
            device_id=(rep, (tp + d) % peers), device_id_type=MESH,
        )
        copy.start()
        tile_sends.append(copy)
    for copy in state_loads:
        copy.wait()
    for copy in tile_sends:
        copy.wait_recv()
    packed = tile_tp[0]
    for d in range(1, peers):
        packed = packed + tile_tp[d]
    tile_rep[0] = packed
    for s in range(1, replicas):
        copy = pltpu.make_async_remote_copy(
            tile_rep.at[0], tile_rep.at[s], r_send.at[s - 1], r_recv.at[s - 1],
            device_id=(rep ^ s, tp), device_id_type=MESH,
        )
        copy.start()
        tile_sends.append(copy)
    for copy in tile_sends[peers - 1 :]:
        copy.wait_recv()
    index = {pair: n for n, pair in enumerate(pairs)}
    seen = [tile_rep[s] for s in range(replicas)]
    gram = {}
    for s, t in pairs:
        value = None
        for d in range(replicas):
            p, q = s ^ d, t ^ d
            picked = jnp.where(lane == index[min(p, q), max(p, q)], seen[d], 0.0)
            value = picked if value is None else value + picked
        gram[s, t] = jnp.sum(value, keepdims=True)
    coef = adasum_weights(gram, replicas)
    coef = [jnp.broadcast_to(coef[s], (SUBLANES, gr.shape[2])) for s in range(replicas)]

    masks = []
    mask = replicas // 2
    while mask:
        masks.append(mask)
        mask //= 2
    piece = rows // PIECES
    outs = []
    w_copies = {}

    def w_send_start(step, s, q):
        m = masks[step]
        at = pl.ds(q * piece, piece)
        copy = pltpu.make_async_remote_copy(
            wb.at[s, at], wb.at[s ^ m, at], w_send.at[s ^ m, q], w_recv.at[s ^ m, q],
            device_id=(rep ^ m, tp), device_id_type=MESH,
        )
        copy.start()
        w_copies[s ^ m, q] = copy

    def put(src, dst, n):
        copy = pltpu.make_async_copy(src, dst, out_sem.at[n])
        copy.start()
        outs.append(copy)

    for q in range(PIECES):
        def update(n, carry):
            at = pl.ds(pl.multiple_of(q * piece + n * SUBLANES * 2, SUBLANES * 2), SUBLANES * 2)
            value = None
            for s in range(replicas):
                term = coef[s][:1] * gr[s, at, :]
                value = term if value is None else value + term
            moment_new = BETA_ONE * moment[at, :] + (1.0 - BETA_ONE) * value
            second_new = BETA_TWO * second[at, :] + (1.0 - BETA_TWO) * value * value
            master_new = master[at, :] - LEARN * (moment_new / CORRECT_ONE) / (
                jnp.sqrt(second_new / CORRECT_TWO) + 1e-08
            )
            comb[at, :] = value
            mom[at, :] = moment_new
            sec[at, :] = second_new
            mas[at, :] = master_new
            wb[0, at, :] = master_new.astype(jnp.bfloat16)
            return carry

        lax.fori_loop(0, piece // (SUBLANES * 2), update, 0)
        for step in range(len(masks)):
            w_send_start(step, 0, q)
    for n, (src, dst) in enumerate(((comb, comb_hbm), (mom, mom_hbm), (sec, sec_hbm), (mas, mas_hbm))):
        put(src, dst, n)
    put(wb.at[0], w_hbm.at[pl.ds(pl.multiple_of(rep * rows, rows), rows)], 4)

    def relay(q, step, s):
        w_copies[s, q].wait_recv()
        for later in range(step + 1, len(masks)):
            w_send_start(later, s, q)

    held = [0]
    for step, m in enumerate(masks):
        fresh = [s ^ m for s in held]
        for q in range(PIECES):
            for s in fresh:
                relay(q, step, s)
        for s in fresh:
            put(wb.at[s], w_hbm.at[pl.ds(pl.multiple_of((rep ^ s) * rows, rows), rows)], 4 + s)
        held = held + fresh

    for cond, copy in pending:
        @pl.when(cond)
        def _():
            copy.wait_send()
    for copy in seg_sends + tile_sends + list(w_copies.values()):
        copy.wait_send()
    for copy in outs:
        copy.wait()


def deliver(*refs):
    sources, targets, buffers, (in_sem, out_sem) = refs[:5], refs[5:10], refs[10:15], refs[15:]
    moves = []
    for n, (src, dst, buf) in enumerate(zip(sources, targets, buffers)):
        step = buf.shape[0] // PIECES
        for q in range(PIECES):
            at = pl.ds(q * step, step)
            load = pltpu.make_async_copy(src.at[at], buf.at[at], in_sem.at[n, q])
            load.start()
            moves.append((load, pltpu.make_async_copy(buf.at[at], dst.at[at], out_sem.at[n, q])))
    for load, store in moves:
        load.wait()
        store.start()
    for _, store in moves:
        store.wait()


def per_device(inputs, cotangent, master, moment, second):
    replicas = lax.axis_size("rep")
    peers = lax.axis_size("tp")
    inner = 1 << (peers.bit_length() - 1) // 2
    outer = peers // inner
    tokens, depth = inputs.shape
    features = cotangent.shape[1]
    rows = depth // replicas
    width = min(LANES, rows)
    chunks = depth // width
    per_segment = rows // width
    shard = jax.ShapeDtypeStruct((rows, features), jnp.float32)
    anywhere = pl.BlockSpec(memory_space=pl.ANY)
    dma = pltpu.SemaphoreType.DMA
    small = pltpu.VMEM((rows, features), jnp.float32)
    results = pl.pallas_call(
        functools.partial(kernel, replicas, outer, inner),
        out_shape=(shard, shard, shard, shard, jax.ShapeDtypeStruct((depth, features), jnp.bfloat16)),
        in_specs=[anywhere] * 5,
        out_specs=(anywhere,) * 5,
        scratch_shapes=[
            pltpu.VMEM((chunks * SPLIT, peers, tokens // SPLIT, width), jnp.bfloat16),
            pltpu.VMEM((SPLIT, cotangent.shape[0] // SPLIT, features), jnp.bfloat16),
            pltpu.VMEM((replicas - 1, rows, features), jnp.float32),
            pltpu.VMEM((replicas, rows, features), jnp.float32),
            small, small, small, small, small, small, small,
            pltpu.VMEM((replicas, rows, features), jnp.bfloat16),
            pltpu.VMEM((peers, SUBLANES, LANES), jnp.float32),
            pltpu.VMEM((replicas, SUBLANES, LANES), jnp.float32),
            dma((chunks * SPLIT,)),
            dma((SPLIT, peers)),
            dma((3,)),
            dma((chunks * SPLIT, 4, peers)),
            dma((chunks * SPLIT, peers)),
            dma((replicas - 1, per_segment)),
            dma((replicas - 1, per_segment)),
            dma((peers - 1,)),
            dma((peers - 1,)),
            dma((replicas - 1,)),
            dma((replicas - 1,)),
            dma((replicas, PIECES)),
            dma((replicas, PIECES)),
            dma((4 + replicas,)),
        ],
        compiler_params=pltpu.CompilerParams(
            collective_id=0, has_side_effects=True, vmem_limit_bytes=60 * 1024 * 1024
        ),
        name="adasum_adam",
    )(inputs, cotangent, master, moment, second)
    return pl.pallas_call(
        deliver,
        out_shape=tuple(jax.ShapeDtypeStruct(r.shape, r.dtype) for r in results),
        in_specs=[anywhere] * 5,
        out_specs=(anywhere,) * 5,
        scratch_shapes=[pltpu.VMEM(r.shape, r.dtype) for r in results] + [dma((5, PIECES)), dma((5, PIECES))],
        compiler_params=pltpu.CompilerParams(vmem_limit_bytes=60 * 1024 * 1024),
        name="deliver",
    )(*results)


def solution(mesh):
    return jax.shard_map(
        per_device,
        mesh=mesh,
        in_specs=(
            P(("rep", "tp"), None),
            P("rep", "tp"),
            P("rep", "tp"),
            P("rep", "tp"),
            P("rep", "tp"),
        ),
        out_specs=(P("rep", "tp"), P("rep", "tp"), P("rep", "tp"), P("rep", "tp"), P(None, "tp")),
        check_vma=False,
    )
```
